32 devices in a mesh: groups: 2 (over y), outer: 2 (over core), inner: 8 (over z, x).
Axes of the slice: x: 2, y: 2, z: 4, core: 2. Of those that a mesh axis runs over, the one named last changes fastest.
Arguments:
- leftover_inputs: bfloat16 [240, 8192], P('groups', ('outer', 'inner')), parts along dimension 0, may hold values from -6 to 6
- codebook_matrix: bfloat16 [8192, 8192], P(('groups', 'outer', 'inner')), parts along dimension 0, may hold values from -0.198873782 to 0.198873782
- remaining_tiles: int32 [32, 2], P(('groups', 'outer', 'inner')), parts along dimension 0, may hold values from 0 to 1, as said below
Outputs:
- screen: float32 [240, 4096], P('groups', ('outer', 'inner')), parts along dimension 0
- coefficients: float32 [240, 4096], P('groups', ('outer', 'inner')), parts along dimension 0
- residual: float32 [240, 8192], P('groups', ('outer', 'inner')), parts along dimension 0
The draws below stay inside these ranges and needn't reach their ends.
There are 2 independent parts, one for each index of `groups`. The reference program is written for one: setup_inputs(seed, part) draws one part's arguments, and reference() takes and returns one part's arrays. A program takes and returns all parts, laid end to end along the dimension named above; each array names one. Nothing has to cross between parts.
Inputs may be any that keep to these rules, and one draw needn't show every extreme that they name: `remaining_tiles`: in every run of 8 devices along inner (one outer index), exactly 2 devices have both blocks surviving and 1 have one.
All inputs are finite; a program needn't handle non-finite values. Where the reference program divides by a largest or mean magnitude, that divisor is 1e-20 or more.
Results may differ from the reference program's by a relative error of at most 0.0019.
Values may be sent and summed in bfloat16 or wider, within the bound.
A program may use at most 128 MiB of HBM per device.

```python
import math
import jax
import jax.numpy as jnp
from jax import lax

W = 8192
GROUP_ELEMENTS = 128
BLK_DEV = 2
TOKENS = 120
ATOMS = 4096
N_OUTER = 2
N_INNER = 8


def draw_codebook_matrix(key, part):
    scale_key, base_key = jax.random.split(key, 2)
    atom_scale = jnp.exp(jax.random.uniform(scale_key, (ATOMS, 1), jnp.float32, math.log(0.3), math.log(3.0)))
    base_values = jnp.clip(jax.random.normal(base_key, (ATOMS, W), jnp.float32), -6.0, 6.0)
    return (base_values * atom_scale / math.sqrt(W)).astype(jnp.bfloat16)


def draw_remaining_tiles(key, part):

    def one_group(group_key):
        order_key, slot_key = jax.random.split(group_key)
        order_rank = jax.random.permutation(order_key, N_INNER)
        slot_pick = jax.random.randint(slot_key, (N_INNER,), 0, 2)
        quarter = N_INNER // 4
        both_alive = order_rank < quarter
        single = (order_rank >= 2 * quarter) & (order_rank < 2 * quarter + N_INNER // 8)
        front_slot = both_alive | single & (slot_pick == 0)
        back_slot = both_alive | single & (slot_pick == 1)
        return jnp.stack([front_slot, back_slot], axis=1).astype(jnp.int32)
    group_rows = jax.vmap(one_group)(jax.random.split(key, N_OUTER))
    return group_rows.reshape(N_OUTER * N_INNER, BLK_DEV)


def shard_levels(key, extent, shards, low, high):
    loudness = 1.0
    for position, shards_of in shards:
        steps = jax.random.uniform(jax.random.fold_in(jax.random.fold_in(key, 6), position), (shards_of,), jnp.float32, low / len(shards), high / len(shards))
        loudness = loudness * jnp.repeat(jnp.exp(steps), extent[position] // shards_of).reshape((-1,) + (1,) * (len(extent) - 1 - position))
    return loudness


def bell_draw(stream_key, dims, deviation, limit, cuts=(), kind=jnp.bfloat16):
    entries = jax.random.normal(stream_key, dims, jnp.float32) * deviation
    if len(cuts) > 0:
        entries = shard_levels(stream_key, dims, cuts, -0.22, 0.18) * entries
    return jnp.clip(entries, min=-limit, max=limit).astype(kind)


def setup_inputs(seed: int = 0, part: int = 0) -> dict:
    streams_of = jax.random.split(jax.random.key(seed), 4)
    part_splits = jax.random.split(jax.random.fold_in(streams_of[3], part), 4)
    return {
        "leftover_inputs": bell_draw(part_splits[0], (TOKENS, W), 1.0, 6.0, ((1, 16),)),
        "codebook_matrix": draw_codebook_matrix(jax.random.fold_in(jax.random.fold_in(streams_of[3], part), 71), part),
        "remaining_tiles": draw_remaining_tiles(jax.random.fold_in(jax.random.fold_in(streams_of[3], part), 71), part),
    }


penalty_ratio = 0.1
epsilon = 1e-06

def shrink(values, threshold):
    return values - jnp.clip(values, -threshold, threshold)

def reference(leftover_inputs, codebook_matrix, remaining_tiles):
    shard_count = N_OUTER * N_INNER
    shard_atoms = BLK_DEV * GROUP_ELEMENTS
    shard_rows = codebook_matrix.reshape(shard_count, shard_atoms, W)

    def correlate(rows_here):
        return lax.dot_general(leftover_inputs, rows_here, (((1,), (1,)), ((), ())), preferred_element_type=jnp.float32)

    def squares(rows_here):
        widened = rows_here.astype(jnp.float32)
        return lax.optimization_barrier(jnp.sum(widened * widened, axis=1))
    correlation = lax.map(correlate, shard_rows)
    correlation = jnp.transpose(correlation, (1, 0, 2)).reshape(TOKENS, ATOMS)
    atom_squares = lax.map(squares, shard_rows).reshape(ATOMS)
    signal_broad = leftover_inputs.astype(jnp.float32)
    energy = lax.optimization_barrier(jnp.sum(signal_broad * signal_broad, axis=1))
    atom_norm = jnp.sqrt(atom_squares + epsilon)
    peak_value = lax.optimization_barrier(jnp.max(jnp.abs(correlation), axis=1)) + epsilon
    widest = jnp.max(atom_squares) + epsilon
    lipschitz = (1.0 + math.sqrt(ATOMS / W)) ** 2 * widest
    radius = (1.0 / penalty_ratio - 1.0) * jnp.sqrt(energy + epsilon)
    screen = (jnp.abs(correlation) + radius[:, None] * atom_norm[None, :]) / peak_value[:, None]
    threshold = (penalty_ratio * peak_value / lipschitz)[:, None]
    retained_element_selector = jnp.repeat(remaining_tiles.reshape(-1).astype(jnp.float32), GROUP_ELEMENTS)[None, :]
    first_step = retained_element_selector * shrink(correlation / lipschitz, threshold)
    first_half = first_step.astype(jnp.bfloat16)
    first_shards = jnp.transpose(first_half.reshape(TOKENS, shard_count, shard_atoms), (1, 0, 2))

    def gather_total(running, paired):
        codes_here, rows_here = paired
        return (running + jnp.dot(codes_here, rows_here, preferred_element_type=jnp.float32), None)
    reconstruction_total, _ = lax.scan(gather_total, jnp.zeros((TOKENS, W), jnp.float32), (first_shards, shard_rows))
    residual = reconstruction_total - signal_broad
    residual_half = residual.astype(jnp.bfloat16)

    def slope_function(rows_here):
        return lax.dot_general(residual_half, rows_here, (((1,), (1,)), ((), ())), preferred_element_type=jnp.float32)
    gradient = lax.map(slope_function, shard_rows)
    gradient = jnp.transpose(gradient, (1, 0, 2)).reshape(TOKENS, ATOMS)
    coefficients = retained_element_selector * shrink(first_step - gradient / lipschitz, threshold)
    return (screen, coefficients, residual)
```

```python
import functools
import math

import jax
import jax.numpy as jnp
from jax import lax
from jax.experimental import pallas as pl
from jax.experimental.pallas import tpu as pltpu
from jax.sharding import PartitionSpec as P

GROUP_ELEMENTS = 128
BLK_DEV = 2


penalty_ratio = 0.1
epsilon = 1e-06


def shrink(values, threshold):
    return values - jnp.clip(values, -threshold, threshold)


def on_device_narrow(leftover_inputs, codebook_matrix, remaining_tiles):
    shard_count = lax.axis_size(("outer", "inner"))
    atoms_local, width = codebook_matrix.shape
    tokens, slab_width = leftover_inputs.shape
    atoms_total = atoms_local * shard_count
    shard_piece = lax.all_gather(leftover_inputs, ("outer", "inner"), axis=1, tiled=True)
    correlation = lax.dot_general(
        shard_piece, codebook_matrix, (((1,), (1,)), ((), ())), preferred_element_type=jnp.float32
    )
    widened = shard_piece.astype(jnp.float32)
    energy = jnp.sum(widened * widened, axis=1)
    whole_signals = shard_piece
    correlation, energy, whole_signals = (correlation, energy, whole_signals)
    atom_squares = jnp.sum(jnp.square(codebook_matrix.astype(jnp.float32)), axis=1)
    local_peak = jnp.max(jnp.abs(correlation), axis=1)
    peak_value, widest = lax.pmax((local_peak, jnp.max(atom_squares)), ("outer", "inner"))
    peak_value = peak_value + epsilon
    lipschitz = (1.0 + math.sqrt(atoms_total / width)) ** 2 * (widest + epsilon)
    atom_norm = jnp.sqrt(atom_squares + epsilon)
    radius = (1.0 / penalty_ratio - 1.0) * jnp.sqrt(energy + epsilon)
    screen = (jnp.abs(correlation) + radius[:, None] * atom_norm[None, :]) / peak_value[:, None]
    threshold = (penalty_ratio * peak_value / lipschitz)[:, None]
    block_rows = codebook_matrix.reshape(BLK_DEV, GROUP_ELEMENTS, width)
    block_corr = correlation.reshape(tokens, BLK_DEV, GROUP_ELEMENTS)
    retained_element_indicators = remaining_tiles[0]
    work_rows = [block_rows[slot_index] for slot_index in range(BLK_DEV)]
    work_corr = [block_corr[:, slot_index] for slot_index in range(BLK_DEV)]
    work_flags = [retained_element_indicators[slot_index] for slot_index in range(BLK_DEV)]

    def first_of(corr_part, keep_flag_value):
        return keep_flag_value.astype(jnp.float32) * shrink(corr_part / lipschitz, threshold)

    def rebuild(first_part, row_portion, keep_flag_value):
        return lax.cond(
            keep_flag_value > 0,
            lambda: jnp.dot(
                first_part.astype(jnp.bfloat16), row_portion, preferred_element_type=jnp.float32
            ),
            lambda: jnp.zeros((tokens, width), jnp.float32),
        )

    first_parts = [
        first_of(work_corr[slot_index], work_flags[slot_index]) for slot_index in range(BLK_DEV)
    ]
    partial_term = rebuild(first_parts[0], work_rows[0], work_flags[0])
    slot_index = 1
    partial_term = partial_term + rebuild(
        first_parts[slot_index], work_rows[slot_index], work_flags[slot_index]
    )
    slab_sum = lax.psum_scatter(partial_term, ("outer", "inner"), scatter_dimension=1, tiled=True)
    residual = slab_sum - leftover_inputs.astype(jnp.float32)
    residual_half = lax.all_gather(
        residual.astype(jnp.bfloat16), ("outer", "inner"), axis=1, tiled=True
    )

    def refine(first_part, row_portion, keep_flag_value):

        def active():
            gradient = lax.dot_general(
                residual_half,
                row_portion,
                (((1,), (1,)), ((), ())),
                preferred_element_type=jnp.float32,
            )
            return keep_flag_value.astype(jnp.float32) * shrink(
                first_part - gradient / lipschitz, threshold
            )

        return lax.cond(
            keep_flag_value > 0, active, lambda: jnp.zeros((tokens, GROUP_ELEMENTS), jnp.float32)
        )

    second_parts = [
        refine(first_parts[slot_index], work_rows[slot_index], work_flags[slot_index])
        for slot_index in range(BLK_DEV)
    ]
    coefficients = jnp.concatenate(second_parts, axis=1)
    return (screen, coefficients, residual)


PIECES = 2
LANES = 128


def fused_kernel(
    ring, width, step_scale,
    x_ref, d_hbm, flags_ref,
    screen_ref, coef_ref, resid_ref,
    d_ref, x_all, r_all, peaks, sib_out, sib_in, right_out, right_in, left_out, left_in,
    load_sem, ag1_send, ag1_recv, ag2_send, ag2_recv,
    peak_send, peak_recv, sib_send, sib_recv, rs_send, rs_recv,
):
    tokens, slab = x_ref.shape
    piece = slab // PIECES
    shards = 2 * ring
    right_hops, left_hops = ring // 2, ring // 2 - 1
    core = lax.axis_index("outer")
    chip = lax.axis_index("inner")
    me = core * ring + chip
    other = 1 - core

    load = pltpu.make_async_copy(d_hbm, d_ref, load_sem)
    load.start()

    barrier = pltpu.get_barrier_semaphore()

    def peer_of(offset):
        peer = lax.rem(me + offset, shards)
        return {"outer": lax.div(peer, ring), "inner": lax.rem(peer, ring)}

    def greet(offset, carry):
        pl.semaphore_signal(
            barrier, inc=1, device_id=peer_of(offset), device_id_type=pl.DeviceIdType.MESH
        )
        return carry

    lax.fori_loop(1, shards, greet, 0)

    place = jnp.where(lax.rem(chip, 2) == 0, lax.div(chip, 2), ring - 1 - lax.div(chip, 2))

    def chip_at(offset):
        spot = lax.rem(place + offset + ring, ring)
        return jnp.where(spot < ring // 2, 2 * spot, 2 * (ring - 1 - spot) + 1)

    to_right = {"outer": core, "inner": chip_at(1)}
    to_left = {"outer": core, "inner": chip_at(-1)}
    to_sibling = {"outer": other, "inner": chip}

    def remote(src, dst, send_sem, recv_sem, target):
        return pltpu.make_async_remote_copy(
            src_ref=src, dst_ref=dst, send_sem=send_sem, recv_sem=recv_sem,
            device_id=target, device_id_type=pl.DeviceIdType.MESH,
        )

    def columns(chunk):
        return d_ref[:, pl.ds(pl.multiple_of(chunk * piece, piece), piece)]

    sent = []

    class Gather:
        def __init__(self, buf, send, recv):
            self.buf, self.send, self.recv = buf, send, recv

        def copy(self, row, part, chunk, target):
            at = self.buf.at[chunk]
            return remote(at, at, self.send.at[row, part], self.recv.at[row, part], target)

        def start(self, row, part, chunk, target):
            made = self.copy(row, part, chunk, target)
            made.start()
            sent.append(made)

        def share(self, slot, part, chunk):
            self.start(right_hops + left_hops + slot, part, chunk, to_sibling)

        def chunk(self, side, offset, part):
            return (side * ring + chip_at(offset)) * PIECES + part

        def begin(self, part):
            mine = self.chunk(core, 0, part)
            self.start(0, part, mine, to_right)
            self.start(right_hops, part, mine, to_left)
            self.share(0, part, mine)

        def run(self, consume):
            for part in range(PIECES):
                consume(self.chunk(core, 0, part))
            shared = [(0, 0)]
            for hop in range(right_hops):
                fresh = []
                for part in range(PIECES):
                    got = self.chunk(core, -1 - hop, part)
                    self.copy(hop, part, got, to_right).wait_recv()
                    if hop + 1 < right_hops:
                        self.start(hop + 1, part, got, to_right)
                    self.share(1 + 2 * hop, part, got)
                    if hop < left_hops:
                        back = self.chunk(core, 1 + hop, part)
                        self.copy(right_hops + hop, part, back, to_left).wait_recv()
                        if hop + 1 < left_hops:
                            self.start(right_hops + hop + 1, part, back, to_left)
                        self.share(2 + 2 * hop, part, back)
                        consume(back)
                    consume(got)
                fresh.append((1 + 2 * hop, -1 - hop))
                if hop < left_hops:
                    fresh.append((2 + 2 * hop, 1 + hop))
                self.take(shared, consume)
                shared = fresh
            self.take(shared, consume)

        def take(self, shared, consume):
            for slot, offset in shared:
                for part in range(PIECES):
                    got = self.chunk(other, offset, part)
                    self.copy(right_hops + left_hops + slot, part, got, to_sibling).wait_recv()
                    consume(got)

    first_gather = Gather(x_all, ag1_send, ag1_recv)
    for part in range(PIECES):
        x_all[me * PIECES + part] = x_ref[:, part * piece:(part + 1) * piece]
    pl.semaphore_wait(barrier, shards - 1)
    for part in range(PIECES):
        first_gather.begin(part)
    load.wait()

    atoms = d_ref.shape[0]

    def add_squares(step, total):
        wide = d_ref[:, pl.ds(pl.multiple_of(step * 512, 512), 512)].astype(jnp.float32)
        wide = wide * wide
        return total + (
            (wide[:, :128] + wide[:, 128:256]) + (wide[:, 256:384] + wide[:, 384:])
        )

    squares = lax.fori_loop(
        0, width // 512, add_squares, jnp.zeros((atoms, LANES), jnp.float32)
    )
    atom_squares = jnp.sum(squares.T, axis=0, keepdims=True)
    atom_norm = jnp.sqrt(atom_squares + epsilon)

    state = {
        "corr": jnp.zeros((tokens, atoms), jnp.float32),
        "energy": jnp.zeros((tokens, LANES), jnp.float32),
        "grad": jnp.zeros((tokens, atoms), jnp.float32),
    }

    def correlate(chunk):
        rows = x_all[chunk]
        state["corr"] = state["corr"] + lax.dot_general(
            rows, columns(chunk), (((1,), (1,)), ((), ())), preferred_element_type=jnp.float32
        )
        wide = rows.astype(jnp.float32)
        wide = wide * wide
        for lane in range(0, piece, LANES):
            state["energy"] = state["energy"] + wide[:, lane:lane + LANES]

    first_gather.run(correlate)
    corr = state["corr"]
    corr_abs = jnp.abs(corr)

    local = jnp.maximum(corr_abs[:, :LANES], corr_abs[:, LANES:])
    local = jnp.concatenate([local, jnp.zeros((LANES - tokens, LANES), jnp.float32)], axis=0)
    peaks[0, 0:1, :] = jnp.max(local.T, axis=0, keepdims=True)
    peaks[0, 1:8, :] = jnp.broadcast_to(
        jnp.maximum(atom_squares[:, :LANES], atom_squares[:, LANES:]), (7, LANES)
    )

    def peak_copy(offset):
        return remote(
            peaks.at[0], peaks.at[offset], peak_send.at[offset], peak_recv.at[offset],
            peer_of(offset),
        )

    def send_peak(offset, carry):
        peak_copy(offset).start()
        return carry

    def take_peak(offset, carry):
        peak_copy(offset).wait_recv()
        return carry

    lax.fori_loop(1, shards, send_peak, 0)
    radius = (1.0 / penalty_ratio - 1.0) * jnp.sqrt(
        jnp.sum(state["energy"], axis=1, keepdims=True) + epsilon
    )
    lax.fori_loop(1, shards, take_peak, 0)
    top = jnp.max(peaks[...], axis=0)
    peak_value = jnp.broadcast_to(top[0:1, :], (LANES, LANES)).T[:tokens, :] + epsilon
    widest = jnp.max(top[1:2, :], axis=1, keepdims=True)
    lipschitz = jnp.broadcast_to(step_scale * (widest + epsilon), (tokens, LANES))
    threshold = penalty_ratio * peak_value / lipschitz
    blocks = range(BLK_DEV)
    keep = [flags_ref[0, block].astype(jnp.float32) for block in blocks]
    lanes = [slice(block * GROUP_ELEMENTS, (block + 1) * GROUP_ELEMENTS) for block in blocks]
    first = [
        keep[block] * shrink(corr[:, lanes[block]] / lipschitz, threshold) for block in blocks
    ]
    codes = jnp.concatenate([part.astype(jnp.bfloat16) for part in first], axis=1)

    def share_of(side, offset, part):
        chunk = (side * ring + chip_at(offset)) * PIECES + part
        return jnp.dot(codes, columns(chunk), preferred_element_type=jnp.float32)

    order = []
    for hop in range(right_hops):
        order.append(right_hops - hop)
        if hop < left_hops:
            order.append(hop - left_hops)
    order.append(0)

    def sib_copy(slot, part):
        return remote(
            sib_out.at[slot, part], sib_in.at[slot, part],
            sib_send.at[slot, part], sib_recv.at[slot, part], to_sibling,
        )

    def offer(slot):
        if slot >= ring:
            return
        for part in range(PIECES):
            sib_out[slot, part] = share_of(other, order[slot], part).astype(jnp.bfloat16)
            made = sib_copy(slot, part)
            made.start()
            sent.append(made)

    def chip_sum(slot, part):
        mine = share_of(core, order[slot], part)
        sib_copy(slot, part).wait_recv()
        return mine + sib_in[slot, part].astype(jnp.float32)

    def ring_copy(out, into, row, hop, part, target):
        return remote(
            out.at[hop, part], into.at[hop, part],
            rs_send.at[row + hop, part], rs_recv.at[row + hop, part], target,
        )

    def pass_on(out, into, row, hop, part, target, slot):
        total = chip_sum(slot, part)
        if hop > 0:
            ring_copy(out, into, row, hop - 1, part, target).wait_recv()
            total = total + into[hop - 1, part].astype(jnp.float32)
        out[hop, part] = total.astype(jnp.bfloat16)
        made = ring_copy(out, into, row, hop, part, target)
        made.start()
        sent.append(made)

    early = min(4, ring)
    for slot in range(early):
        offer(slot)
    for hop in range(right_hops):
        for part in range(PIECES):
            pass_on(right_out, right_in, 0, hop, part, to_right, order.index(right_hops - hop))
            if hop < left_hops:
                pass_on(
                    left_out, left_in, right_hops, hop, part, to_left,
                    order.index(hop - left_hops),
                )
        offer(early + 2 * hop)
        offer(early + 2 * hop + 1)
        if hop == 0:
            for block in blocks:
                screen_ref[:, lanes[block]] = (
                    corr_abs[:, lanes[block]] + radius * atom_norm[:, lanes[block]]
                ) / peak_value

    second_gather = Gather(r_all, ag2_send, ag2_recv)
    for part in range(PIECES):
        total = chip_sum(ring - 1, part)
        ring_copy(right_out, right_in, 0, right_hops - 1, part, to_right).wait_recv()
        total = total + right_in[right_hops - 1, part].astype(jnp.float32)
        ring_copy(left_out, left_in, right_hops, left_hops - 1, part, to_left).wait_recv()
        total = total + left_in[left_hops - 1, part].astype(jnp.float32)
        here = slice(part * piece, (part + 1) * piece)
        residual = total - x_ref[:, here].astype(jnp.float32)
        resid_ref[:, here] = residual
        r_all[me * PIECES + part] = residual.astype(jnp.bfloat16)
        second_gather.begin(part)

    def descend(chunk):
        state["grad"] = state["grad"] + lax.dot_general(
            r_all[chunk], columns(chunk), (((1,), (1,)), ((), ())),
            preferred_element_type=jnp.float32,
        )

    second_gather.run(descend)
    for block in blocks:
        coef_ref[:, lanes[block]] = keep[block] * shrink(
            first[block] - state["grad"][:, lanes[block]] / lipschitz, threshold
        )

    for made in sent:
        made.wait_send()

    def close_peak(offset, carry):
        peak_copy(offset).wait_send()
        return carry

    lax.fori_loop(1, shards, close_peak, 0)


def on_device(leftover_inputs, codebook_matrix, remaining_tiles):
    ring, cores = lax.axis_size("inner"), lax.axis_size("outer")
    tokens, slab = leftover_inputs.shape
    atoms, width = codebook_matrix.shape
    wide_enough = slab % (PIECES * LANES) == 0 and width % 512 == 0
    if not (wide_enough and cores == 2 and ring % 2 == 0 and ring >= 4 and tokens <= LANES):
        return on_device_narrow(leftover_inputs, codebook_matrix, remaining_tiles)
    shards = cores * ring
    piece = slab // PIECES
    hops = ring - 1
    step_scale = (1.0 + math.sqrt(atoms * shards / width)) ** 2
    vmem = pl.BlockSpec(memory_space=pltpu.VMEM)
    dma = pltpu.SemaphoreType.DMA

    def block(*lead):
        return pltpu.VMEM((*lead, tokens, piece), jnp.bfloat16)

    return pl.pallas_call(
        functools.partial(fused_kernel, ring, width, step_scale),
        out_shape=(
            jax.ShapeDtypeStruct((tokens, atoms), jnp.float32),
            jax.ShapeDtypeStruct((tokens, atoms), jnp.float32),
            jax.ShapeDtypeStruct((tokens, slab), jnp.float32),
        ),
        in_specs=[
            vmem,
            pl.BlockSpec(memory_space=pl.ANY),
            pl.BlockSpec(memory_space=pltpu.SMEM),
        ],
        out_specs=(vmem, vmem, vmem),
        scratch_shapes=[
            pltpu.VMEM((atoms, width), jnp.bfloat16),
            block(shards * PIECES),
            block(shards * PIECES),
            pltpu.VMEM((shards, 8, LANES), jnp.float32),
            block(ring, PIECES),
            block(ring, PIECES),
            block(ring // 2, PIECES),
            block(ring // 2, PIECES),
            block(ring // 2 - 1, PIECES),
            block(ring // 2 - 1, PIECES),
            dma,
            dma((hops + ring, PIECES)),
            dma((hops + ring, PIECES)),
            dma((hops + ring, PIECES)),
            dma((hops + ring, PIECES)),
            dma((shards,)),
            dma((shards,)),
            dma((ring, PIECES)),
            dma((ring, PIECES)),
            dma((hops, PIECES)),
            dma((hops, PIECES)),
        ],
        compiler_params=pltpu.CompilerParams(
            collective_id=0, has_side_effects=True, vmem_limit_bytes=40 << 20
        ),
    )(leftover_inputs, codebook_matrix, remaining_tiles)


def solution(mesh):
    in_specs = (
        P("groups", ("outer", "inner")),
        P(("groups", "outer", "inner"), None),
        P(("groups", "outer", "inner"), None),
    )
    out_specs = (
        P("groups", ("outer", "inner")),
        P("groups", ("outer", "inner")),
        P("groups", ("outer", "inner")),
    )
    return jax.shard_map(
        on_device, mesh=mesh, in_specs=in_specs, out_specs=out_specs, check_vma=False
    )
```

```python
import functools
import math

import jax
import jax.numpy as jnp
from jax import lax
from jax.experimental import pallas as pl
from jax.experimental.pallas import tpu as pltpu
from jax.sharding import PartitionSpec as P

GROUP_ELEMENTS = 128
BLK_DEV = 2


penalty_ratio = 0.1
epsilon = 1e-06


def shrink(values, threshold):
    return values - jnp.clip(values, -threshold, threshold)


def on_device_narrow(leftover_inputs, codebook_matrix, remaining_tiles):
    shard_count = lax.axis_size(("outer", "inner"))
    atoms_local, width = codebook_matrix.shape
    tokens, slab_width = leftover_inputs.shape
    atoms_total = atoms_local * shard_count
    shard_piece = lax.all_gather(leftover_inputs, ("outer", "inner"), axis=1, tiled=True)
    correlation = lax.dot_general(
        shard_piece, codebook_matrix, (((1,), (1,)), ((), ())), preferred_element_type=jnp.float32
    )
    widened = shard_piece.astype(jnp.float32)
    energy = jnp.sum(widened * widened, axis=1)
    whole_signals = shard_piece
    correlation, energy, whole_signals = (correlation, energy, whole_signals)
    atom_squares = jnp.sum(jnp.square(codebook_matrix.astype(jnp.float32)), axis=1)
    local_peak = jnp.max(jnp.abs(correlation), axis=1)
    peak_value, widest = lax.pmax((local_peak, jnp.max(atom_squares)), ("outer", "inner"))
    peak_value = peak_value + epsilon
    lipschitz = (1.0 + math.sqrt(atoms_total / width)) ** 2 * (widest + epsilon)
    atom_norm = jnp.sqrt(atom_squares + epsilon)
    radius = (1.0 / penalty_ratio - 1.0) * jnp.sqrt(energy + epsilon)
    screen = (jnp.abs(correlation) + radius[:, None] * atom_norm[None, :]) / peak_value[:, None]
    threshold = (penalty_ratio * peak_value / lipschitz)[:, None]
    block_rows = codebook_matrix.reshape(BLK_DEV, GROUP_ELEMENTS, width)
    block_corr = correlation.reshape(tokens, BLK_DEV, GROUP_ELEMENTS)
    retained_element_indicators = remaining_tiles[0]
    work_rows = [block_rows[slot_index] for slot_index in range(BLK_DEV)]
    work_corr = [block_corr[:, slot_index] for slot_index in range(BLK_DEV)]
    work_flags = [retained_element_indicators[slot_index] for slot_index in range(BLK_DEV)]

    def first_of(corr_part, keep_flag_value):
        return keep_flag_value.astype(jnp.float32) * shrink(corr_part / lipschitz, threshold)

    def rebuild(first_part, row_portion, keep_flag_value):
        return lax.cond(
            keep_flag_value > 0,
            lambda: jnp.dot(
                first_part.astype(jnp.bfloat16), row_portion, preferred_element_type=jnp.float32
            ),
            lambda: jnp.zeros((tokens, width), jnp.float32),
        )

    first_parts = [
        first_of(work_corr[slot_index], work_flags[slot_index]) for slot_index in range(BLK_DEV)
    ]
    partial_term = rebuild(first_parts[0], work_rows[0], work_flags[0])
    slot_index = 1
    partial_term = partial_term + rebuild(
        first_parts[slot_index], work_rows[slot_index], work_flags[slot_index]
    )
    slab_sum = lax.psum_scatter(partial_term, ("outer", "inner"), scatter_dimension=1, tiled=True)
    residual = slab_sum - leftover_inputs.astype(jnp.float32)
    residual_half = lax.all_gather(
        residual.astype(jnp.bfloat16), ("outer", "inner"), axis=1, tiled=True
    )

    def refine(first_part, row_portion, keep_flag_value):

        def active():
            gradient = lax.dot_general(
                residual_half,
                row_portion,
                (((1,), (1,)), ((), ())),
                preferred_element_type=jnp.float32,
            )
            return keep_flag_value.astype(jnp.float32) * shrink(
                first_part - gradient / lipschitz, threshold
            )

        return lax.cond(
            keep_flag_value > 0, active, lambda: jnp.zeros((tokens, GROUP_ELEMENTS), jnp.float32)
        )

    second_parts = [
        refine(first_parts[slot_index], work_rows[slot_index], work_flags[slot_index])
        for slot_index in range(BLK_DEV)
    ]
    coefficients = jnp.concatenate(second_parts, axis=1)
    return (screen, coefficients, residual)


PIECES = 4
LANES = 128


def fused_kernel(
    ring, width, step_scale,
    x_hbm, d_hbm, flags_hbm,
    screen_ref, coef_ref, resid_ref,
    d_ref, flags_ref, squares, x_all, r_all, peaks, sib_out, sib_in, right_out, right_in, left_out, left_in,
    load_sem, x_sem, flag_sem, ag1_send, ag1_recv, ag2_send, ag2_recv,
    peak_send, peak_recv, sib_send, sib_recv, rs_send, rs_recv,
):
    tokens, slab = x_hbm.shape
    piece = slab // PIECES
    shards = 2 * ring
    half_ring = ring // 2

    def goes_right(hop, part):
        return hop < half_ring - 1 or (hop < half_ring and part < PIECES // 2)

    def goes_left(hop, part):
        return hop < half_ring - 1 or (hop < half_ring and part >= PIECES // 2)

    core = lax.axis_index("outer")
    chip = lax.axis_index("inner")
    me = core * ring + chip
    other = 1 - core

    x_loads = [
        pltpu.make_async_copy(
            x_hbm.at[:, pl.ds(part * piece, piece)], x_all.at[me * PIECES + part], x_sem.at[part]
        )
        for part in range(PIECES)
    ]
    for made in x_loads:
        made.start()

    barrier = pltpu.get_barrier_semaphore()

    def peer_of(offset):
        peer = lax.rem(me + offset, shards)
        return {"outer": lax.div(peer, ring), "inner": lax.rem(peer, ring)}

    place = jnp.where(lax.rem(chip, 2) == 0, lax.div(chip, 2), ring - 1 - lax.div(chip, 2))

    def chip_at(offset):
        spot = lax.rem(place + offset + ring, ring)
        return jnp.where(spot < ring // 2, 2 * spot, 2 * (ring - 1 - spot) + 1)

    to_right = {"outer": core, "inner": chip_at(1)}
    to_left = {"outer": core, "inner": chip_at(-1)}
    to_sibling = {"outer": other, "inner": chip}

    for target in (to_right, to_left, to_sibling):
        pl.semaphore_signal(
            barrier, inc=1, device_id=target, device_id_type=pl.DeviceIdType.MESH
        )
    load = pltpu.make_async_copy(d_hbm, d_ref, load_sem)
    load.start()
    flag_load = pltpu.make_async_copy(flags_hbm, flags_ref, flag_sem)
    flag_load.start()

    def remote(src, dst, send_sem, recv_sem, target):
        return pltpu.make_async_remote_copy(
            src_ref=src, dst_ref=dst, send_sem=send_sem, recv_sem=recv_sem,
            device_id=target, device_id_type=pl.DeviceIdType.MESH,
        )

    def columns(chunk):
        return d_ref[:, pl.ds(pl.multiple_of(chunk * piece, piece), piece)]

    sent = []

    class Gather:
        def __init__(self, buf, send, recv):
            self.buf, self.send, self.recv = buf, send, recv

        def copy(self, row, part, chunk, target):
            at = self.buf.at[chunk]
            return remote(at, at, self.send.at[row, part], self.recv.at[row, part], target)

        def start(self, row, part, chunk, target):
            made = self.copy(row, part, chunk, target)
            made.start()
            sent.append(made)

        def share(self, slot, part, chunk):
            self.start(2 * half_ring + slot, part, chunk, to_sibling)

        def chunk(self, side, offset, part):
            return (side * ring + chip_at(offset)) * PIECES + part

        def begin(self, part):
            mine = self.chunk(core, 0, part)
            if goes_right(0, part):
                self.start(0, part, mine, to_right)
            if goes_left(0, part):
                self.start(half_ring, part, mine, to_left)
            self.share(0, part, mine)

        def run(self, consume):
            for part in range(PIECES):
                consume(self.chunk(core, 0, part))
            shared = [(0, 0, part) for part in range(PIECES)]
            for hop in range(half_ring):
                fresh = []
                for part in range(PIECES):
                    landed = []
                    for goes, row, sign, target in (
                        (goes_right, 0, -1, to_right), (goes_left, half_ring, 1, to_left)
                    ):
                        if not goes(hop, part):
                            continue
                        offset = sign * (1 + hop)
                        got = self.chunk(core, offset, part)
                        self.copy(row + hop, part, got, target).wait_recv()
                        if goes(hop + 1, part):
                            self.start(row + hop + 1, part, got, target)
                        slot = min(1 + 2 * hop + (sign > 0), ring - 1)
                        self.share(slot, part, got)
                        fresh.append((slot, offset, part))
                        landed.append(got)
                    for got in landed:
                        consume(got)
                self.take(shared, consume)
                shared = fresh
            self.take(shared, consume)

        def take(self, shared, consume):
            for slot, offset, part in shared:
                got = self.chunk(other, offset, part)
                self.copy(2 * half_ring + slot, part, got, to_sibling).wait_recv()
                consume(got)

    first_gather = Gather(x_all, ag1_send, ag1_recv)
    pl.semaphore_wait(barrier, 3)
    for part in range(PIECES):
        x_loads[part].wait()
        first_gather.begin(part)
    squares[...] = jnp.zeros_like(squares)
    flag_load.wait()
    load.wait()

    atoms = d_ref.shape[0]
    state = {
        "corr": jnp.zeros((tokens, atoms), jnp.float32),
        "energy": jnp.zeros((tokens, LANES), jnp.float32),
        "grad": jnp.zeros((tokens, atoms), jnp.float32),
    }

    def correlate(chunk):
        rows, held = x_all[chunk], columns(chunk)
        state["corr"] = state["corr"] + lax.dot_general(
            rows, held, (((1,), (1,)), ((), ())), preferred_element_type=jnp.float32
        )
        broad = held.astype(jnp.float32)
        broad = broad * broad
        squares[...] += sum(broad[:, lane:lane + LANES] for lane in range(0, piece, LANES))
        wide = rows.astype(jnp.float32)
        wide = wide * wide
        for lane in range(0, piece, LANES):
            state["energy"] = state["energy"] + wide[:, lane:lane + LANES]

    first_gather.run(correlate)
    corr = state["corr"]
    corr_abs = jnp.abs(corr)
    atom_squares = jnp.sum(squares[...].T, axis=0, keepdims=True)
    atom_norm = jnp.sqrt(atom_squares + epsilon)

    local = jnp.maximum(corr_abs[:, :LANES], corr_abs[:, LANES:])
    local = jnp.concatenate([local, jnp.zeros((LANES - tokens, LANES), jnp.float32)], axis=0)
    peaks[0, 0:1, :] = jnp.max(local.T, axis=0, keepdims=True)
    peaks[0, 1:8, :] = jnp.broadcast_to(
        jnp.maximum(atom_squares[:, :LANES], atom_squares[:, LANES:]), (7, LANES)
    )

    def peak_copy(offset):
        return remote(
            peaks.at[0], peaks.at[offset], peak_send.at[offset], peak_recv.at[offset],
            peer_of(offset),
        )

    def send_peak(offset, carry):
        peak_copy(offset).start()
        return carry

    def take_peak(offset, carry):
        peak_copy(offset).wait_recv()
        return carry

    lax.fori_loop(1, shards, send_peak, 0)
    radius = (1.0 / penalty_ratio - 1.0) * jnp.sqrt(
        jnp.sum(state["energy"], axis=1, keepdims=True) + epsilon
    )
    lax.fori_loop(1, shards, take_peak, 0)
    top = jnp.max(peaks[...], axis=0)
    peak_value = jnp.broadcast_to(top[0:1, :], (LANES, LANES)).T[:tokens, :] + epsilon
    widest = jnp.max(top[1:2, :], axis=1, keepdims=True)
    lipschitz = jnp.broadcast_to(step_scale * (widest + epsilon), (tokens, LANES))
    threshold = penalty_ratio * peak_value / lipschitz
    blocks = range(BLK_DEV)
    keep = [flags_ref[0, block].astype(jnp.float32) for block in blocks]
    lanes = [slice(block * GROUP_ELEMENTS, (block + 1) * GROUP_ELEMENTS) for block in blocks]
    first = [
        keep[block] * shrink(corr[:, lanes[block]] / lipschitz, threshold) for block in blocks
    ]
    codes = jnp.concatenate([part.astype(jnp.bfloat16) for part in first], axis=1)

    def share_of(side, offset, part):
        chunk = (side * ring + chip_at(offset)) * PIECES + part
        return jnp.dot(codes, columns(chunk), preferred_element_type=jnp.float32)

    order = [half_ring]
    for away in range(half_ring - 1, 0, -1):
        order += [away, -away]
    order.append(0)

    def sib_copy(slot, part):
        return remote(
            sib_out.at[slot, part], sib_in.at[slot, part],
            sib_send.at[slot, part], sib_recv.at[slot, part], to_sibling,
        )

    def offer(slot):
        if slot >= ring:
            return
        for part in range(PIECES):
            sib_out[slot, part] = share_of(other, order[slot], part).astype(jnp.bfloat16)
            made = sib_copy(slot, part)
            made.start()
            sent.append(made)

    def chip_sum(slot, part):
        mine = share_of(core, order[slot], part)
        sib_copy(slot, part).wait_recv()
        return mine + sib_in[slot, part].astype(jnp.float32)

    def ring_copy(out, into, row, hop, part, target):
        return remote(
            out.at[hop, part], into.at[hop, part],
            rs_send.at[row + hop, part], rs_recv.at[row + hop, part], target,
        )

    ways = (
        (goes_right, right_out, right_in, 0, 1, to_right),
        (goes_left, left_out, left_in, half_ring, -1, to_left),
    )

    def starts_at(goes, part):
        return 0 if goes(half_ring - 1, part) else 1

    def pass_on(way, hop, part):
        goes, out, into, row, sign, target = way
        first_hop = starts_at(goes, part)
        if hop < first_hop:
            return
        away = half_ring - hop
        slot = order.index(away if away == half_ring else sign * away)
        total = chip_sum(slot, part)
        if hop > first_hop:
            ring_copy(out, into, row, hop - 1, part, target).wait_recv()
            total = total + into[hop - 1, part].astype(jnp.float32)
        out[hop, part] = total.astype(jnp.bfloat16)
        made = ring_copy(out, into, row, hop, part, target)
        made.start()
        sent.append(made)

    early = min(3, ring)
    for slot in range(early):
        offer(slot)
    for hop in range(half_ring):
        for part in range(PIECES):
            for way in ways:
                pass_on(way, hop, part)
        offer(early + 2 * hop)
        offer(early + 2 * hop + 1)
        if hop == 0:
            for block in blocks:
                screen_ref[:, lanes[block]] = (
                    corr_abs[:, lanes[block]] + radius * atom_norm[:, lanes[block]]
                ) / peak_value

    second_gather = Gather(r_all, ag2_send, ag2_recv)
    for part in range(PIECES):
        total = chip_sum(ring - 1, part)
        for goes, out, into, row, sign, target in ways:
            ring_copy(out, into, row, half_ring - 1, part, target).wait_recv()
            total = total + into[half_ring - 1, part].astype(jnp.float32)
        here = slice(part * piece, (part + 1) * piece)
        residual = total - x_all[me * PIECES + part].astype(jnp.float32)
        resid_ref[:, here] = residual
        r_all[me * PIECES + part] = residual.astype(jnp.bfloat16)
        second_gather.begin(part)

    def descend(chunk):
        state["grad"] = state["grad"] + lax.dot_general(
            r_all[chunk], columns(chunk), (((1,), (1,)), ((), ())),
            preferred_element_type=jnp.float32,
        )

    second_gather.run(descend)
    for block in blocks:
        coef_ref[:, lanes[block]] = keep[block] * shrink(
            first[block] - state["grad"][:, lanes[block]] / lipschitz, threshold
        )

    for made in sent:
        made.wait_send()

    def close_peak(offset, carry):
        peak_copy(offset).wait_send()
        return carry

    lax.fori_loop(1, shards, close_peak, 0)


def on_device(leftover_inputs, codebook_matrix, remaining_tiles):
    ring, cores = lax.axis_size("inner"), lax.axis_size("outer")
    tokens, slab = leftover_inputs.shape
    atoms, width = codebook_matrix.shape
    wide_enough = slab % (PIECES * LANES) == 0 and width % 512 == 0
    if not (wide_enough and cores == 2 and ring % 2 == 0 and ring >= 4 and tokens <= LANES):
        return on_device_narrow(leftover_inputs, codebook_matrix, remaining_tiles)
    shards = cores * ring
    piece = slab // PIECES
    hops = ring
    step_scale = (1.0 + math.sqrt(atoms * shards / width)) ** 2
    vmem = pl.BlockSpec(memory_space=pltpu.VMEM)
    dma = pltpu.SemaphoreType.DMA

    def block(*lead):
        return pltpu.VMEM((*lead, tokens, piece), jnp.bfloat16)

    return pl.pallas_call(
        functools.partial(fused_kernel, ring, width, step_scale),
        out_shape=(
            jax.ShapeDtypeStruct((tokens, atoms), jnp.float32),
            jax.ShapeDtypeStruct((tokens, atoms), jnp.float32),
            jax.ShapeDtypeStruct((tokens, slab), jnp.float32),
        ),
        in_specs=[
            pl.BlockSpec(memory_space=pl.ANY),
            pl.BlockSpec(memory_space=pl.ANY),
            pl.BlockSpec(memory_space=pl.ANY),
        ],
        out_specs=(vmem, vmem, vmem),
        scratch_shapes=[
            pltpu.VMEM((atoms, width), jnp.bfloat16),
            pltpu.SMEM((1, BLK_DEV), jnp.int32),
            pltpu.VMEM((atoms, LANES), jnp.float32),
            block(shards * PIECES),
            block(shards * PIECES),
            pltpu.VMEM((shards, 8, LANES), jnp.float32),
            block(ring, PIECES),
            block(ring, PIECES),
            block(ring // 2, PIECES),
            block(ring // 2, PIECES),
            block(ring // 2, PIECES),
            block(ring // 2, PIECES),
            dma,
            dma((PIECES,)),
            dma,
            dma((hops + ring, PIECES)),
            dma((hops + ring, PIECES)),
            dma((hops + ring, PIECES)),
            dma((hops + ring, PIECES)),
            dma((shards,)),
            dma((shards,)),
            dma((ring, PIECES)),
            dma((ring, PIECES)),
            dma((hops, PIECES)),
            dma((hops, PIECES)),
        ],
        compiler_params=pltpu.CompilerParams(
            collective_id=0, has_side_effects=True, vmem_limit_bytes=40 << 20
        ),
    )(leftover_inputs, codebook_matrix, remaining_tiles)


def solution(mesh):
    in_specs = (
        P("groups", ("outer", "inner")),
        P(("groups", "outer", "inner"), None),
        P(("groups", "outer", "inner"), None),
    )
    out_specs = (
        P("groups", ("outer", "inner")),
        P("groups", ("outer", "inner")),
        P("groups", ("outer", "inner")),
    )
    return jax.shard_map(
        on_device, mesh=mesh, in_specs=in_specs, out_specs=out_specs, check_vma=False
    )
```

```python
import functools
import math

import jax
import jax.numpy as jnp
from jax import lax
from jax.experimental import pallas as pl
from jax.experimental.pallas import tpu as pltpu
from jax.sharding import PartitionSpec as P

GROUP_ELEMENTS = 128
BLK_DEV = 2


penalty_ratio = 0.1
epsilon = 1e-06


def shrink(values, threshold):
    return values - jnp.clip(values, -threshold, threshold)


def on_device_narrow(leftover_inputs, codebook_matrix, remaining_tiles):
    shard_count = lax.axis_size(("outer", "inner"))
    atoms_local, width = codebook_matrix.shape
    tokens, slab_width = leftover_inputs.shape
    atoms_total = atoms_local * shard_count
    shard_piece = lax.all_gather(leftover_inputs, ("outer", "inner"), axis=1, tiled=True)
    correlation = lax.dot_general(
        shard_piece, codebook_matrix, (((1,), (1,)), ((), ())), preferred_element_type=jnp.float32
    )
    widened = shard_piece.astype(jnp.float32)
    energy = jnp.sum(widened * widened, axis=1)
    whole_signals = shard_piece
    correlation, energy, whole_signals = (correlation, energy, whole_signals)
    atom_squares = jnp.sum(jnp.square(codebook_matrix.astype(jnp.float32)), axis=1)
    local_peak = jnp.max(jnp.abs(correlation), axis=1)
    peak_value, widest = lax.pmax((local_peak, jnp.max(atom_squares)), ("outer", "inner"))
    peak_value = peak_value + epsilon
    lipschitz = (1.0 + math.sqrt(atoms_total / width)) ** 2 * (widest + epsilon)
    atom_norm = jnp.sqrt(atom_squares + epsilon)
    radius = (1.0 / penalty_ratio - 1.0) * jnp.sqrt(energy + epsilon)
    screen = (jnp.abs(correlation) + radius[:, None] * atom_norm[None, :]) / peak_value[:, None]
    threshold = (penalty_ratio * peak_value / lipschitz)[:, None]
    block_rows = codebook_matrix.reshape(BLK_DEV, GROUP_ELEMENTS, width)
    block_corr = correlation.reshape(tokens, BLK_DEV, GROUP_ELEMENTS)
    retained_element_indicators = remaining_tiles[0]
    work_rows = [block_rows[slot_index] for slot_index in range(BLK_DEV)]
    work_corr = [block_corr[:, slot_index] for slot_index in range(BLK_DEV)]
    work_flags = [retained_element_indicators[slot_index] for slot_index in range(BLK_DEV)]

    def first_of(corr_part, keep_flag_value):
        return keep_flag_value.astype(jnp.float32) * shrink(corr_part / lipschitz, threshold)

    def rebuild(first_part, row_portion, keep_flag_value):
        return lax.cond(
            keep_flag_value > 0,
            lambda: jnp.dot(
                first_part.astype(jnp.bfloat16), row_portion, preferred_element_type=jnp.float32
            ),
            lambda: jnp.zeros((tokens, width), jnp.float32),
        )

    first_parts = [
        first_of(work_corr[slot_index], work_flags[slot_index]) for slot_index in range(BLK_DEV)
    ]
    partial_term = rebuild(first_parts[0], work_rows[0], work_flags[0])
    slot_index = 1
    partial_term = partial_term + rebuild(
        first_parts[slot_index], work_rows[slot_index], work_flags[slot_index]
    )
    slab_sum = lax.psum_scatter(partial_term, ("outer", "inner"), scatter_dimension=1, tiled=True)
    residual = slab_sum - leftover_inputs.astype(jnp.float32)
    residual_half = lax.all_gather(
        residual.astype(jnp.bfloat16), ("outer", "inner"), axis=1, tiled=True
    )

    def refine(first_part, row_portion, keep_flag_value):

        def active():
            gradient = lax.dot_general(
                residual_half,
                row_portion,
                (((1,), (1,)), ((), ())),
                preferred_element_type=jnp.float32,
            )
            return keep_flag_value.astype(jnp.float32) * shrink(
                first_part - gradient / lipschitz, threshold
            )

        return lax.cond(
            keep_flag_value > 0, active, lambda: jnp.zeros((tokens, GROUP_ELEMENTS), jnp.float32)
        )

    second_parts = [
        refine(first_parts[slot_index], work_rows[slot_index], work_flags[slot_index])
        for slot_index in range(BLK_DEV)
    ]
    coefficients = jnp.concatenate(second_parts, axis=1)
    return (screen, coefficients, residual)


PIECES = 4
LANES = 128


def fused_kernel(
    ring, width, step_scale,
    x_hbm, d_hbm, flags_hbm,
    screen_ref, coef_ref, resid_ref,
    d_ref, flags_ref, squares, x_all, r_all, peaks, sib_out, sib_in, right_out, right_in, left_out, left_in,
    load_sem, x_sem, flag_sem, ag1_send, ag1_recv, ag2_send, ag2_recv,
    peak_send, peak_recv, sib_send, sib_recv, rs_send, rs_recv,
):
    tokens, slab = x_hbm.shape
    piece = slab // PIECES
    shards = 2 * ring
    half_ring = ring // 2

    def goes_right(hop, part):
        return hop < half_ring - 1 or (hop < half_ring and part < PIECES // 2)

    def goes_left(hop, part):
        return hop < half_ring - 1 or (hop < half_ring and part >= PIECES // 2)

    core = lax.axis_index("outer")
    chip = lax.axis_index("inner")
    me = core * ring + chip
    other = 1 - core

    x_loads = [
        pltpu.make_async_copy(
            x_hbm.at[:, pl.ds(part * piece, piece)], x_all.at[me * PIECES + part], x_sem.at[part]
        )
        for part in range(PIECES)
    ]
    for made in x_loads:
        made.start()

    barrier = pltpu.get_barrier_semaphore()

    def peer_of(offset):
        peer = lax.rem(me + offset, shards)
        return {"outer": lax.div(peer, ring), "inner": lax.rem(peer, ring)}

    place = jnp.where(lax.rem(chip, 2) == 0, lax.div(chip, 2), ring - 1 - lax.div(chip, 2))

    def chip_at(offset):
        spot = lax.rem(place + offset + ring, ring)
        return jnp.where(spot < ring // 2, 2 * spot, 2 * (ring - 1 - spot) + 1)

    to_right = {"outer": core, "inner": chip_at(1)}
    to_left = {"outer": core, "inner": chip_at(-1)}
    to_sibling = {"outer": other, "inner": chip}

    for target in (to_right, to_left, to_sibling):
        pl.semaphore_signal(
            barrier, inc=1, device_id=target, device_id_type=pl.DeviceIdType.MESH
        )
    load = pltpu.make_async_copy(d_hbm, d_ref, load_sem)
    load.start()
    flag_load = pltpu.make_async_copy(flags_hbm, flags_ref, flag_sem)
    flag_load.start()

    def remote(src, dst, send_sem, recv_sem, target):
        return pltpu.make_async_remote_copy(
            src_ref=src, dst_ref=dst, send_sem=send_sem, recv_sem=recv_sem,
            device_id=target, device_id_type=pl.DeviceIdType.MESH,
        )

    def columns(chunk):
        return d_ref[:, pl.ds(pl.multiple_of(chunk * piece, piece), piece)]

    sent = []

    class Gather:
        def __init__(self, buf, send, recv):
            self.buf, self.send, self.recv = buf, send, recv

        def copy(self, row, part, chunk, target):
            at = self.buf.at[chunk]
            return remote(at, at, self.send.at[row, part], self.recv.at[row, part], target)

        def start(self, row, part, chunk, target):
            made = self.copy(row, part, chunk, target)
            made.start()
            sent.append(made)

        def share(self, slot, part, chunk):
            self.start(2 * half_ring + slot, part, chunk, to_sibling)

        def chunk(self, side, offset, part):
            return (side * ring + chip_at(offset)) * PIECES + part

        def begin(self, part):
            mine = self.chunk(core, 0, part)
            if goes_right(0, part):
                self.start(0, part, mine, to_right)
            if goes_left(0, part):
                self.start(half_ring, part, mine, to_left)

        def run(self, consume):
            for part in range(PIECES):
                self.share(0, part, self.chunk(core, 0, part))
            for part in range(PIECES):
                consume(self.chunk(core, 0, part))
            shared = [(0, 0, part) for part in range(PIECES)]
            for hop in range(half_ring):
                fresh = []
                for part in range(PIECES):
                    landed = []
                    for goes, row, sign, target in (
                        (goes_right, 0, -1, to_right), (goes_left, half_ring, 1, to_left)
                    ):
                        if not goes(hop, part):
                            continue
                        offset = sign * (1 + hop)
                        got = self.chunk(core, offset, part)
                        self.copy(row + hop, part, got, target).wait_recv()
                        if goes(hop + 1, part):
                            self.start(row + hop + 1, part, got, target)
                        slot = min(1 + 2 * hop + (sign > 0), ring - 1)
                        self.share(slot, part, got)
                        fresh.append((slot, offset, part))
                        landed.append(got)
                    for got in landed:
                        consume(got)
                self.take(shared, consume)
                shared = fresh
            self.take(shared, consume)

        def take(self, shared, consume):
            for slot, offset, part in shared:
                got = self.chunk(other, offset, part)
                self.copy(2 * half_ring + slot, part, got, to_sibling).wait_recv()
                consume(got)

    first_gather = Gather(x_all, ag1_send, ag1_recv)
    pl.semaphore_wait(barrier, 3)
    for part in range(PIECES):
        x_loads[part].wait()
        first_gather.begin(part)
    squares[...] = jnp.zeros_like(squares)
    flag_load.wait()
    load.wait()

    atoms = d_ref.shape[0]
    state = {
        "corr": jnp.zeros((tokens, atoms), jnp.float32),
        "energy": jnp.zeros((tokens, LANES), jnp.float32),
        "grad": jnp.zeros((tokens, atoms), jnp.float32),
    }

    def correlate(chunk):
        rows, held = x_all[chunk], columns(chunk)
        state["corr"] = state["corr"] + lax.dot_general(
            rows, held, (((1,), (1,)), ((), ())), preferred_element_type=jnp.float32
        )
        broad = held.astype(jnp.float32)
        broad = broad * broad
        squares[...] += sum(broad[:, lane:lane + LANES] for lane in range(0, piece, LANES))
        wide = rows.astype(jnp.float32)
        wide = wide * wide
        for lane in range(0, piece, LANES):
            state["energy"] = state["energy"] + wide[:, lane:lane + LANES]

    first_gather.run(correlate)
    corr = state["corr"]
    corr_abs = jnp.abs(corr)
    atom_squares = jnp.sum(squares[...].T, axis=0, keepdims=True)
    atom_norm = jnp.sqrt(atom_squares + epsilon)

    local = jnp.maximum(corr_abs[:, :LANES], corr_abs[:, LANES:])
    local = jnp.concatenate([local, jnp.zeros((LANES - tokens, LANES), jnp.float32)], axis=0)
    peaks[0, 0:1, :] = jnp.max(local.T, axis=0, keepdims=True)
    peaks[0, 1:8, :] = jnp.broadcast_to(
        jnp.maximum(atom_squares[:, :LANES], atom_squares[:, LANES:]), (7, LANES)
    )

    def peak_copy(offset):
        return remote(
            peaks.at[0], peaks.at[offset], peak_send.at[offset], peak_recv.at[offset],
            peer_of(offset),
        )

    def send_peak(offset, carry):
        peak_copy(offset).start()
        return carry

    def take_peak(offset, carry):
        peak_copy(offset).wait_recv()
        return carry

    lax.fori_loop(1, shards, send_peak, 0)
    radius = (1.0 / penalty_ratio - 1.0) * jnp.sqrt(
        jnp.sum(state["energy"], axis=1, keepdims=True) + epsilon
    )
    lax.fori_loop(1, shards, take_peak, 0)
    top = jnp.max(peaks[...], axis=0)
    peak_value = jnp.broadcast_to(top[0:1, :], (LANES, LANES)).T[:tokens, :] + epsilon
    widest = jnp.max(top[1:2, :], axis=1, keepdims=True)
    lipschitz = jnp.broadcast_to(step_scale * (widest + epsilon), (tokens, LANES))
    threshold = penalty_ratio * peak_value / lipschitz
    blocks = range(BLK_DEV)
    keep = [flags_ref[0, block].astype(jnp.float32) for block in blocks]
    lanes = [slice(block * GROUP_ELEMENTS, (block + 1) * GROUP_ELEMENTS) for block in blocks]
    first = [
        keep[block] * shrink(corr[:, lanes[block]] / lipschitz, threshold) for block in blocks
    ]
    codes = jnp.concatenate([part.astype(jnp.bfloat16) for part in first], axis=1)

    def share_of(side, offset, part):
        chunk = (side * ring + chip_at(offset)) * PIECES + part
        return jnp.dot(codes, columns(chunk), preferred_element_type=jnp.float32)

    order = [half_ring]
    for away in range(half_ring - 1, 0, -1):
        order += [away, -away]
    order.append(0)

    def sib_copy(slot, part):
        return remote(
            sib_out.at[slot, part], sib_in.at[slot, part],
            sib_send.at[slot, part], sib_recv.at[slot, part], to_sibling,
        )

    def offer(slot):
        if slot >= ring:
            return
        for part in range(PIECES):
            sib_out[slot, part] = share_of(other, order[slot], part).astype(jnp.bfloat16)
            made = sib_copy(slot, part)
            made.start()
            sent.append(made)

    def chip_sum(slot, part):
        mine = share_of(core, order[slot], part)
        sib_copy(slot, part).wait_recv()
        return mine + sib_in[slot, part].astype(jnp.float32)

    def ring_copy(out, into, row, hop, part, target):
        return remote(
            out.at[hop, part], into.at[hop, part],
            rs_send.at[row + hop, part], rs_recv.at[row + hop, part], target,
        )

    ways = (
        (goes_right, right_out, right_in, 0, 1, to_right),
        (goes_left, left_out, left_in, half_ring, -1, to_left),
    )

    def starts_at(goes, part):
        return 0 if goes(half_ring - 1, part) else 1

    def pass_on(way, hop, part):
        goes, out, into, row, sign, target = way
        first_hop = starts_at(goes, part)
        if hop < first_hop:
            return
        away = half_ring - hop
        slot = order.index(away if away == half_ring else sign * away)
        total = chip_sum(slot, part)
        if hop > first_hop:
            ring_copy(out, into, row, hop - 1, part, target).wait_recv()
            total = total + into[hop - 1, part].astype(jnp.float32)
        out[hop, part] = total.astype(jnp.bfloat16)
        made = ring_copy(out, into, row, hop, part, target)
        made.start()
        sent.append(made)

    early = min(3, ring)
    for slot in range(early):
        offer(slot)
    for hop in range(half_ring):
        for part in range(PIECES):
            for way in ways:
                pass_on(way, hop, part)
        offer(early + 2 * hop)
        offer(early + 2 * hop + 1)

    second_gather = Gather(r_all, ag2_send, ag2_recv)
    for part in range(PIECES):
        total = chip_sum(ring - 1, part)
        for goes, out, into, row, sign, target in ways:
            ring_copy(out, into, row, half_ring - 1, part, target).wait_recv()
            total = total + into[half_ring - 1, part].astype(jnp.float32)
        here = slice(part * piece, (part + 1) * piece)
        residual = total - x_all[me * PIECES + part].astype(jnp.float32)
        resid_ref[:, here] = residual
        r_all[me * PIECES + part] = residual.astype(jnp.bfloat16)
        second_gather.begin(part)

    def descend(chunk):
        state["grad"] = state["grad"] + lax.dot_general(
            r_all[chunk], columns(chunk), (((1,), (1,)), ((), ())),
            preferred_element_type=jnp.float32,
        )

    for block in blocks:
        screen_ref[:, lanes[block]] = (
            corr_abs[:, lanes[block]] + radius * atom_norm[:, lanes[block]]
        ) / peak_value
    second_gather.run(descend)
    for block in blocks:
        coef_ref[:, lanes[block]] = keep[block] * shrink(
            first[block] - state["grad"][:, lanes[block]] / lipschitz, threshold
        )

    for made in sent:
        made.wait_send()

    def close_peak(offset, carry):
        peak_copy(offset).wait_send()
        return carry

    lax.fori_loop(1, shards, close_peak, 0)


def on_device(leftover_inputs, codebook_matrix, remaining_tiles):
    ring, cores = lax.axis_size("inner"), lax.axis_size("outer")
    tokens, slab = leftover_inputs.shape
    atoms, width = codebook_matrix.shape
    wide_enough = slab % (PIECES * LANES) == 0 and width % 512 == 0
    if not (wide_enough and cores == 2 and ring % 2 == 0 and ring >= 4 and tokens <= LANES):
        return on_device_narrow(leftover_inputs, codebook_matrix, remaining_tiles)
    shards = cores * ring
    piece = slab // PIECES
    hops = ring
    step_scale = (1.0 + math.sqrt(atoms * shards / width)) ** 2
    vmem = pl.BlockSpec(memory_space=pltpu.VMEM)
    dma = pltpu.SemaphoreType.DMA

    def block(*lead):
        return pltpu.VMEM((*lead, tokens, piece), jnp.bfloat16)

    return pl.pallas_call(
        functools.partial(fused_kernel, ring, width, step_scale),
        out_shape=(
            jax.ShapeDtypeStruct((tokens, atoms), jnp.float32),
            jax.ShapeDtypeStruct((tokens, atoms), jnp.float32),
            jax.ShapeDtypeStruct((tokens, slab), jnp.float32),
        ),
        in_specs=[
            pl.BlockSpec(memory_space=pl.ANY),
            pl.BlockSpec(memory_space=pl.ANY),
            pl.BlockSpec(memory_space=pl.ANY),
        ],
        out_specs=(vmem, vmem, vmem),
        scratch_shapes=[
            pltpu.VMEM((atoms, width), jnp.bfloat16),
            pltpu.SMEM((1, BLK_DEV), jnp.int32),
            pltpu.VMEM((atoms, LANES), jnp.float32),
            block(shards * PIECES),
            block(shards * PIECES),
            pltpu.VMEM((shards, 8, LANES), jnp.float32),
            block(ring, PIECES),
            block(ring, PIECES),
            block(ring // 2, PIECES),
            block(ring // 2, PIECES),
            block(ring // 2, PIECES),
            block(ring // 2, PIECES),
            dma,
            dma((PIECES,)),
            dma,
            dma((hops + ring, PIECES)),
            dma((hops + ring, PIECES)),
            dma((hops + ring, PIECES)),
            dma((hops + ring, PIECES)),
            dma((shards,)),
            dma((shards,)),
            dma((ring, PIECES)),
            dma((ring, PIECES)),
            dma((hops, PIECES)),
            dma((hops, PIECES)),
        ],
        compiler_params=pltpu.CompilerParams(
            collective_id=0, has_side_effects=True, vmem_limit_bytes=40 << 20
        ),
    )(leftover_inputs, codebook_matrix, remaining_tiles)


def solution(mesh):
    in_specs = (
        P("groups", ("outer", "inner")),
        P(("groups", "outer", "inner"), None),
        P(("groups", "outer", "inner"), None),
    )
    out_specs = (
        P("groups", ("outer", "inner")),
        P("groups", ("outer", "inner")),
        P("groups", ("outer", "inner")),
    )
    return jax.shard_map(
        on_device, mesh=mesh, in_specs=in_specs, out_specs=out_specs, check_vma=False
    )
```
